32 devices in a mesh: dp: 8 (over y, x, core), seq: 4 (over z).
Axes of the slice: x: 2, y: 2, z: 4, core: 2. Of those that a mesh axis runs over, the one named last changes fastest.
Arguments:
- inputs: bfloat16 [16, 576, 1152], P('dp', 'seq'), may hold values from -90 to 90
- cotangent: bfloat16 [16, 576, 1152], P('dp', 'seq'), may hold values from -6 to 6
- ln1_gain: bfloat16 [1152], P(('dp', 'seq')), may hold values from 0.099609375 to 1.8984375
- ln1_bias: bfloat16 [1152], P(('dp', 'seq')), may hold values from -3 to 3
- qkv_weight: bfloat16 [1152, 3456], P(('dp', 'seq')), may hold values from -0.1875 to 0.1875
- qv_bias: bfloat16 [2, 1152], P(None, ('dp', 'seq')), may hold values from -3 to 3
- out_weight: bfloat16 [1152, 1152], P(('dp', 'seq')), may hold values from -2.5 to 2.5
- out_bias: bfloat16 [1152], P(('dp', 'seq')), may hold values from -3 to 3
- ln2_gain: bfloat16 [1152], P(('dp', 'seq')), may hold values from 0.099609375 to 1.8984375
- ln2_bias: bfloat16 [1152], P(('dp', 'seq')), may hold values from -3 to 3
- up_weight: bfloat16 [1152, 4304], P(('dp', 'seq')), may hold values from -0.1875 to 0.1875
- up_bias: bfloat16 [4304], replicated, may hold values from -3 to 3
- down_weight: bfloat16 [4304, 1152], P(None, ('dp', 'seq')), may hold values from -0.09375 to 0.09375
- down_bias: bfloat16 [1152], P(('dp', 'seq')), may hold values from -3 to 3
Outputs:
- output: bfloat16 [16, 576, 1152], P('dp', 'seq')
- input_grad: bfloat16 [16, 576, 1152], P('dp', 'seq')
- ln1_gain_grad: float32 [1152], P(('dp', 'seq'))
- ln1_bias_grad: float32 [1152], P(('dp', 'seq'))
- qkv_weight_grad: float32 [1152, 3456], P(('dp', 'seq'))
- qv_bias_grad: float32 [2, 1152], P(None, ('dp', 'seq'))
- out_weight_grad: float32 [1152, 1152], P(('dp', 'seq'))
- out_bias_grad: float32 [1152], P(('dp', 'seq'))
- ln2_gain_grad: float32 [1152], P(('dp', 'seq'))
- ln2_bias_grad: float32 [1152], P(('dp', 'seq'))
- up_weight_grad: float32 [1152, 4304], P(('dp', 'seq'))
- up_bias_grad: float32 [4304], replicated
- down_weight_grad: float32 [4304, 1152], P(None, ('dp', 'seq'))
- down_bias_grad: float32 [1152], P(('dp', 'seq'))
The draws below stay inside these ranges and needn't reach their ends.
All inputs are finite; a program needn't handle non-finite values.
Results may differ from the reference program's by a relative error of at most 0.012.
The reference program's roundings to bfloat16 on the way count: a program that leaves them out, or rounds other values in their place, can miss the bound.
Values may be sent and summed in bfloat16 or wider, within the bound.
No kernel may reach another device: no remote copies, remote signals or barrier semaphores. Data moves between devices by JAX's collectives and lax.ppermute only.
A program may use at most 320 MiB of HBM per device.

```python
import math
import jax
import jax.numpy as jnp
from jax import lax

HEADS = 16
HEAD = 72
D = 1152
FF = 4304
LEN = 576
IMAGES = 16


def draw_inputs(key, part):
    core_key = jax.random.fold_in(key, 11)
    row_key = jax.random.fold_in(key, 12)
    column_key = jax.random.fold_in(key, 13)
    row_scale = jnp.exp(jax.random.uniform(row_key, (IMAGES, LEN, 1), jnp.float32, 0.0, math.log(10.0)))
    column_scale = jnp.exp(jax.random.uniform(column_key, (1, 1, D), jnp.float32, math.log(0.3), math.log(3.0)))
    core_part = jnp.clip(jax.random.normal(core_key, (IMAGES, LEN, D), jnp.float32), -3.0, 3.0)
    return (core_part * row_scale * column_scale).astype(jnp.bfloat16)


def levels(key, extent, split, smallest, largest):
    def one(axis_at, blocks):
        steps = jax.random.uniform(jax.random.fold_in(jax.random.fold_in(key, 6), axis_at), (blocks,), jnp.float32, smallest / len(split), largest / len(split))
        return jnp.repeat(jnp.exp(steps), extent[axis_at] // blocks).reshape((-1,) + (1,) * (len(extent) - axis_at - 1))

    gain = one(*split[0])
    for cut in split[1:]:
        gain = gain * one(*cut)
    return gain


def bell_draw(rng, shape, scale, bound, cuts=(), kind=jnp.bfloat16):
    gain = levels(rng, shape, cuts, -0.22, 0.18) if cuts else 1.0
    entries = jax.random.normal(rng, shape, jnp.float32) * scale * gain
    return jnp.minimum(jnp.maximum(entries, -bound), bound).astype(kind)


def setup_inputs(seed: int = 0) -> dict:
    key_of = jax.random.split(jax.random.key(seed), 15)
    inputs = draw_inputs(jax.random.fold_in(key_of[14], 71), 0)
    cotangent = bell_draw(key_of[1], (IMAGES, LEN, D), 1.0, 6.0, ((0, 8), (1, 4)))
    ln1_gain = jnp.clip(1.0 + 0.18 * jax.random.normal(key_of[2], (D,), jnp.float32), 0.099609375, 1.8984375).astype(jnp.bfloat16)
    ln1_bias = bell_draw(key_of[3], (D,), 0.5, 3.0, ((0, 32),))
    qkv_weight = bell_draw(key_of[4], (D, 3 * D), D ** -0.5, 0.1875, ((0, 32),))
    qv_bias = bell_draw(key_of[5], (2, D), 0.5, 3.0, ((1, 32),))
    out_weight = bell_draw(key_of[6], (D, D), (max(1, 3 * D // LEN)) ** -0.5, 2.5, ((0, 32),))
    out_bias = bell_draw(key_of[7], (D,), 0.5, 3.0, ((0, 32),))
    ln2_gain = jnp.clip(1.0 + 0.18 * jax.random.normal(key_of[8], (D,), jnp.float32), 0.099609375, 1.8984375).astype(jnp.bfloat16)
    ln2_bias = bell_draw(key_of[9], (D,), 0.5, 3.0, ((0, 32),))
    up_weight = bell_draw(key_of[10], (D, FF), D ** -0.5, 0.1875, ((0, 32),))
    up_bias = bell_draw(key_of[11], (FF,), 0.5, 3.0)
    down_weight = bell_draw(key_of[12], (FF, D), FF ** -0.5, 0.09375, ((1, 32),))
    down_bias = bell_draw(key_of[13], (D,), 0.5, 3.0, ((0, 32),))
    return {"inputs": inputs, "cotangent": cotangent, "ln1_gain": ln1_gain, "ln1_bias": ln1_bias, "qkv_weight": qkv_weight, "qv_bias": qv_bias, "out_weight": out_weight, "out_bias": out_bias, "ln2_gain": ln2_gain, "ln2_bias": ln2_bias, "up_weight": up_weight, "up_bias": up_bias, "down_weight": down_weight, "down_bias": down_bias}


EPS = 1e-06
GELU_C = 0.7978845608028654
GELU_A = 0.044715

def rounded(values):
    return lax.optimization_barrier(values.astype(jnp.bfloat16)).astype(jnp.float32)

def layer_norm(values, gain_row, offset):
    average = lax.optimization_barrier(jnp.mean(values, axis=-1, keepdims=True))
    centred = values - average
    variance = lax.optimization_barrier(jnp.mean(centred * centred, axis=-1, keepdims=True))
    inverse = lax.rsqrt(variance + EPS)
    normed = centred * inverse
    return (normed, inverse, normed * gain_row + offset)

def norm_back(grad_normed, normed, inverse):
    mean_grad = lax.optimization_barrier(jnp.mean(grad_normed, axis=-1, keepdims=True))
    mean_mixed = lax.optimization_barrier(jnp.mean(grad_normed * normed, axis=-1, keepdims=True))
    return inverse * (grad_normed - mean_grad - normed * mean_mixed)

def gelu_parts(pre_act):
    inner_arg = GELU_C * (pre_act + GELU_A * pre_act * pre_act * pre_act)
    tangent = jnp.tanh(inner_arg)
    gelu_value = 0.5 * pre_act * (1.0 + tangent)
    slopes = 0.5 * (1.0 + tangent) + 0.5 * pre_act * (1.0 - tangent * tangent) * GELU_C * (1.0 + 3.0 * GELU_A * pre_act * pre_act)
    return (gelu_value, slopes)

def attend_ref(queries, key_rows, value_rows, scaling, block_rows):
    length, head_count, head_width = queries.shape
    query_f = queries.astype(jnp.float32)
    key_f = key_rows.astype(jnp.float32)
    value_f = value_rows.astype(jnp.float32)

    def one_block(block_index):
        query_block = lax.dynamic_slice_in_dim(query_f, (block_index * block_rows).astype(jnp.int32), block_rows, 0)
        scores = jnp.einsum('qhd,khd->hqk', query_block, key_f) * scaling
        row_top = lax.optimization_barrier(jnp.max(scores, axis=-1, keepdims=True))
        row_total = lax.optimization_barrier(jnp.sum(jnp.exp(scores - row_top), axis=-1, keepdims=True))
        log_total = row_top + jnp.log(row_total)
        probabilities = rounded(jnp.exp(scores - log_total))
        attended = jnp.einsum('hqk,khd->qhd', probabilities, value_f).astype(jnp.bfloat16)
        return (attended, log_total[:, :, 0])
    attended, log_total = lax.map(one_block, jnp.arange(length // block_rows, dtype=jnp.int32))
    return (attended.reshape(length, head_count, head_width), jnp.moveaxis(log_total, 0, 1).reshape(head_count, length))

def attend_back_ref(queries, key_rows, value_rows, attended, log_total, grad_attended, scaling, block_rows):
    length, head_count, head_width = queries.shape
    query_f = queries.astype(jnp.float32)
    key_f = key_rows.astype(jnp.float32)
    value_f = value_rows.astype(jnp.float32)
    grad_f = grad_attended.astype(jnp.float32)
    row_delta = lax.optimization_barrier(jnp.sum(grad_f * attended.astype(jnp.float32), axis=-1))

    def one_block(running, block_index):
        key_grad, value_grad = running
        row_start = (block_index * block_rows).astype(jnp.int32)
        query_block = lax.dynamic_slice_in_dim(query_f, row_start, block_rows, 0)
        grad_block = lax.dynamic_slice_in_dim(grad_f, row_start, block_rows, 0)
        log_block = lax.dynamic_slice_in_dim(log_total, row_start, block_rows, 1)
        delta_block = lax.dynamic_slice_in_dim(row_delta, row_start, block_rows, 0)
        scores = jnp.einsum('qhd,khd->hqk', query_block, key_f) * scaling
        probabilities = jnp.exp(scores - log_block[:, :, None])
        value_grad = value_grad + jnp.einsum('hqk,qhd->khd', rounded(probabilities), grad_block)
        prob_grad = jnp.einsum('qhd,khd->hqk', grad_block, value_f)
        score_grad = rounded(probabilities * (prob_grad - jnp.transpose(delta_block)[:, :, None]) * scaling)
        query_grad = jnp.einsum('hqk,khd->qhd', score_grad, key_f)
        key_grad = key_grad + jnp.einsum('hqk,qhd->khd', score_grad, query_block)
        return ((key_grad, value_grad), query_grad)
    zero_grad = jnp.zeros((length, head_count, head_width), jnp.float32)
    (key_grad, value_grad), query_grad = lax.scan(one_block, (zero_grad, zero_grad), jnp.arange(length // block_rows, dtype=jnp.int32))
    return (query_grad.reshape(length, head_count, head_width), key_grad, value_grad)

def image_pass(one_image, grad_image, weights_all):
    ln1_gain, ln1_bias, qkv_weight, qv_bias, out_weight, out_bias, ln2_gain, ln2_bias, up_weight, up_bias, down_weight, down_bias = weights_all
    length = one_image.shape[0]
    width = HEADS * HEAD
    scaling = HEAD ** (-0.5)
    block_rows = min(576, length)
    gain_one = ln1_gain.astype(jnp.float32)
    gain_two = ln2_gain.astype(jnp.float32)
    input_f = one_image.astype(jnp.float32)
    normed1, inverse1, shifted1 = layer_norm(input_f, gain_one, ln1_bias.astype(jnp.float32))
    attn_input = shifted1.astype(jnp.bfloat16)
    bias_full = jnp.concatenate([qv_bias[0].astype(jnp.float32), jnp.zeros((width,), jnp.float32), qv_bias[1].astype(jnp.float32)])
    projected = (jnp.dot(attn_input, qkv_weight, preferred_element_type=jnp.float32) + bias_full).astype(jnp.bfloat16)
    queries = projected[:, :width].reshape(length, HEADS, HEAD)
    key_rows = projected[:, width:2 * width].reshape(length, HEADS, HEAD)
    value_rows = projected[:, 2 * width:].reshape(length, HEADS, HEAD)
    attended, log_total = attend_ref(queries, key_rows, value_rows, scaling, block_rows)
    attended_flat = attended.reshape(length, width)
    hidden = input_f + jnp.dot(attended_flat, out_weight, preferred_element_type=jnp.float32) + out_bias.astype(jnp.float32)
    normed2, inverse2, shifted2 = layer_norm(hidden, gain_two, ln2_bias.astype(jnp.float32))
    mlp_input = shifted2.astype(jnp.bfloat16)
    pre_act = jnp.dot(mlp_input, up_weight, preferred_element_type=jnp.float32) + up_bias.astype(jnp.float32)
    gelu_value, slopes = gelu_parts(pre_act)
    gelu_out = gelu_value.astype(jnp.bfloat16)
    result = (hidden + jnp.dot(gelu_out, down_weight, preferred_element_type=jnp.float32) + down_bias.astype(jnp.float32)).astype(jnp.bfloat16)
    grad_f = grad_image.astype(jnp.float32)
    down_bias_grad = lax.optimization_barrier(jnp.sum(grad_f, axis=0))
    down_weight_grad = jnp.dot(gelu_out.T, grad_image, preferred_element_type=jnp.float32)
    gelu_grad = jnp.dot(grad_image, down_weight.T, preferred_element_type=jnp.float32)
    pre_grad = (gelu_grad * slopes).astype(jnp.bfloat16)
    up_weight_grad = jnp.dot(mlp_input.T, pre_grad, preferred_element_type=jnp.float32)
    up_bias_grad = lax.optimization_barrier(jnp.sum(pre_grad.astype(jnp.float32), axis=0))
    mlp_in_grad = jnp.dot(pre_grad, up_weight.T, preferred_element_type=jnp.float32)
    ln2_gain_grad = lax.optimization_barrier(jnp.sum(mlp_in_grad * normed2, axis=0))
    ln2_bias_grad = lax.optimization_barrier(jnp.sum(mlp_in_grad, axis=0))
    hidden_grad = grad_f + norm_back(mlp_in_grad * gain_two, normed2, inverse2)
    out_bias_grad = lax.optimization_barrier(jnp.sum(hidden_grad, axis=0))
    hidden_grad_b = hidden_grad.astype(jnp.bfloat16)
    out_weight_grad = jnp.dot(attended_flat.T, hidden_grad_b, preferred_element_type=jnp.float32)
    attended_grad = jnp.dot(hidden_grad_b, out_weight.T, preferred_element_type=jnp.float32).astype(jnp.bfloat16).reshape(length, HEADS, HEAD)
    query_grad, key_grad, value_grad = attend_back_ref(queries, key_rows, value_rows, attended, log_total, attended_grad, scaling, block_rows)
    projected_grad = jnp.concatenate([query_grad.reshape(length, width), key_grad.reshape(length, width), value_grad.reshape(length, width)], axis=1).astype(jnp.bfloat16)
    qkv_weight_grad = jnp.dot(attn_input.T, projected_grad, preferred_element_type=jnp.float32)
    projected_f = projected_grad.astype(jnp.float32)
    qv_bias_grad = jnp.stack([lax.optimization_barrier(jnp.sum(projected_f[:, :width], axis=0)), lax.optimization_barrier(jnp.sum(projected_f[:, 2 * width:], axis=0))])
    attn_in_grad = jnp.dot(projected_grad, qkv_weight.T, preferred_element_type=jnp.float32)
    ln1_gain_grad = lax.optimization_barrier(jnp.sum(attn_in_grad * normed1, axis=0))
    ln1_bias_grad = lax.optimization_barrier(jnp.sum(attn_in_grad, axis=0))
    input_grad = (hidden_grad + norm_back(attn_in_grad * gain_one, normed1, inverse1)).astype(jnp.bfloat16)
    grads = (ln1_gain_grad, ln1_bias_grad, qkv_weight_grad, qv_bias_grad, out_weight_grad, out_bias_grad, ln2_gain_grad, ln2_bias_grad, up_weight_grad, up_bias_grad, down_weight_grad, down_bias_grad)
    return (result, input_grad, grads)

def reference(inputs, cotangent, ln1_gain, ln1_bias, qkv_weight, qv_bias, out_weight, out_bias, ln2_gain, ln2_bias, up_weight, up_bias, down_weight, down_bias):
    weights_all = (ln1_gain, ln1_bias, qkv_weight, qv_bias, out_weight, out_bias, ln2_gain, ln2_bias, up_weight, up_bias, down_weight, down_bias)

    def per_image(totals, one_pair):
        one_image, grad_image = one_pair
        result, input_grad, grads = image_pass(one_image, grad_image, weights_all)
        return (tuple((left + right for left, right in zip(totals, grads))), (result, input_grad))
    zero_totals = tuple((jnp.zeros(weight.shape, jnp.float32) for weight in weights_all))
    totals, (results, input_grads) = lax.scan(per_image, zero_totals, (inputs, cotangent))
    return (results, input_grads, totals[0], totals[1], totals[2], totals[3], totals[4], totals[5], totals[6], totals[7], totals[8], totals[9], totals[10], totals[11])
```

```python
import functools
import math

import jax
import jax.numpy as jnp
from jax import lax
from jax.experimental import pallas as pl
from jax.experimental.pallas import tpu as pltpu
from jax.sharding import PartitionSpec as P

HEADS = 16
HEAD = 72
EPS = 1e-06
GELU_C = 0.7978845608028654
GELU_A = 0.044715
LANES = 128
AXES = ("chip", "core", "seq")
F32 = jnp.float32
BF16 = jnp.bfloat16


def nn(left, right):
    return lax.dot_general(left, right, (((1,), (0,)), ((), ())), preferred_element_type=F32)


def nt(left, right):
    return lax.dot_general(left, right, (((1,), (1,)), ((), ())), preferred_element_type=F32)


def tn(left, right):
    return lax.dot_general(left, right, (((0,), (0,)), ((), ())), preferred_element_type=F32)


def norm_stats(values):
    average = jnp.mean(values, axis=-1, keepdims=True)
    centred = values - average
    variance = jnp.mean(centred * centred, axis=-1, keepdims=True)
    inverse = lax.rsqrt(variance + EPS)
    return centred * inverse, inverse


def norm_back(grad_normed, normed, inverse):
    mean_grad = jnp.mean(grad_normed, axis=-1, keepdims=True)
    mean_mixed = jnp.mean(grad_normed * normed, axis=-1, keepdims=True)
    return inverse * (grad_normed - mean_grad - normed * mean_mixed)


def gelu_parts(pre_act):
    inner_arg = GELU_C * (pre_act + GELU_A * pre_act * pre_act * pre_act)
    tangent = jnp.tanh(inner_arg)
    gelu_value = 0.5 * pre_act * (1.0 + tangent)
    slopes = 0.5 * (1.0 + tangent) + 0.5 * pre_act * (1.0 - tangent * tangent) * GELU_C * (
        1.0 + 3.0 * GELU_A * pre_act * pre_act
    )
    return gelu_value, slopes


class Grid:
    def __init__(self, dps, seqs):
        self.dps, self.seqs = dps, seqs
        self.chips = dps // 2
        self.chip, self.core = lax.axis_index("chip"), lax.axis_index("core")
        self.seq = lax.axis_index("seq")

    def flat(self, chip, core, seq):
        return (chip * 2 + core) * self.seqs + seq

    def pairs(self, where):
        out = []
        for chip in range(self.chips):
            for core in range(2):
                for seq in range(self.seqs):
                    out.append((self.flat(chip, core, seq), self.flat(*where(chip, core, seq))))
        return out

    def send(self, value, where):
        return lax.ppermute(value, AXES, self.pairs(where))

    def swap_core(self, value):
        return self.send(value, lambda p, c, s: (p, 1 - c, s))

    def swap_chip(self, value, bit):
        return self.send(value, lambda p, c, s: (p ^ bit, c, s))

    def swap_seq(self, value, bit):
        return self.send(value, lambda p, c, s: (p, c, s ^ bit))

    def by_core(self, mine, other, axis):
        first = self.core == 0
        return jnp.concatenate(
            [jnp.where(first, mine, other), jnp.where(first, other, mine)], axis=axis
        )

    def join(self, mine, axis):
        return self.by_core(mine, self.swap_core(mine), axis)


def bits_of(count):
    return [1 << b for b in reversed(range(count.bit_length() - 1))]


def home_of(grid, images):
    span = grid.seqs // (2 * images)

    def target(step):
        def where(chip, core, seq):
            image = (step + seq) % 2
            owner = core * 2 + image
            return chip, (seq // 2) % 2, owner * span + seq // 4

        return where

    return target


def to_home(grid, values):
    images = values.shape[0]
    target = home_of(grid, images)
    span = grid.seqs // (2 * images)
    got = []
    for step in range(2):
        pick = lax.dynamic_index_in_dim(values, (step + grid.seq) % 2, 0, keepdims=False)
        got.append(grid.send(pick, target(step)))
    even = (grid.seq // span) % 2 == 0
    return jnp.concatenate(
        [jnp.where(even, got[0], got[1]), jnp.where(even, got[1], got[0])], axis=0
    )


def from_home(grid, values, images):
    target = home_of(grid, images)
    span = grid.seqs // (2 * images)
    tokens = values.shape[0] // 2
    odd = (grid.seq // span) % 2
    got = []
    for step in range(2):
        slot = (odd + step) % 2
        piece = lax.dynamic_slice_in_dim(values, slot * tokens, tokens, 0)
        got.append(
            lax.ppermute(piece, AXES, [(b, a) for a, b in grid.pairs(target(step))])
        )
    even = grid.seq % 2 == 0
    return jnp.stack([jnp.where(even, got[0], got[1]), jnp.where(even, got[1], got[0])])


def take_bit(value, shape, bit_value):
    return lax.dynamic_index_in_dim(value.reshape(shape), bit_value, 1, keepdims=False)


def scatter_sum(grid, grad, rows):
    chips, seqs = grid.chips, grid.seqs
    width = grad.shape[-1]
    block = rows * seqs
    parts = grad.reshape(chips, 2, block, width)
    done = []
    for colour in range(2):
        current = parts[:, colour]
        order = bits_of(chips)
        if colour:
            order = order[::-1]
        left = list(bits_of(chips))
        for bit in order:
            at = left.index(bit)
            hi, lo = 1 << at, 1 << (len(left) - at - 1)
            shape = (hi, 2, lo, block, width)
            mine = (grid.chip // bit) % 2
            outgoing = take_bit(current, shape, 1 - mine)
            kept = take_bit(current, shape, mine)
            arrived = grid.swap_chip(outgoing, bit)
            current = (kept.astype(F32) + arrived.astype(F32)).astype(BF16)
            left.remove(bit)
        done.append(current.reshape(seqs, rows, width))
    current = jnp.stack(done)
    count = seqs
    for bit in bits_of(seqs):
        shape = (2, 2, count // 2, rows, width)
        mine = (grid.seq // bit) % 2
        outgoing = lax.dynamic_index_in_dim(current.reshape(shape), 1 - mine, 1, keepdims=False)
        kept = lax.dynamic_index_in_dim(current.reshape(shape), mine, 1, keepdims=False)
        arrived = grid.swap_seq(outgoing.astype(BF16), bit)
        current = kept.astype(F32) + arrived.astype(F32)
        count //= 2
        if count > 1:
            current = current.astype(BF16)
    return current.reshape(2, rows, width)


def own_rows(grid, summed):
    mine = lax.dynamic_index_in_dim(summed, grid.core, 0, keepdims=False)
    other = lax.dynamic_index_in_dim(summed, 1 - grid.core, 0, keepdims=False)
    arrived = grid.swap_core(other)
    first = grid.core == 0
    return jnp.where(first, mine, arrived), jnp.where(first, arrived, mine)


def all_sum(grid, value):
    value = value + grid.swap_core(value)
    for bit in bits_of(grid.chips):
        value = value + grid.swap_chip(value, bit)
    for bit in bits_of(grid.seqs):
        value = value + grid.swap_seq(value, bit)
    return value


def head_cols(ref, base, head):
    start = base + head * HEAD
    return ref[:, start : start + HEAD]


def pad_lanes(value):
    return jnp.concatenate(
        [value, jnp.zeros((value.shape[0], LANES - value.shape[1]), value.dtype)], axis=1
    )


def attend_kernel(heads, spans, scaling, *refs):
    proj = refs[0]
    extra = refs[1 : 1 + spans]
    out, lse = refs[1 + spans : 3 + spans]
    q_t, k_s, v_t, o_t = refs[3 + spans :]
    tokens = proj.shape[0]
    flat = heads * HEAD
    scale2 = scaling * math.log2(math.e)
    for head in range(heads):
        q_t[head] = jnp.transpose(pad_lanes(head_cols(proj, 0, head)))
        k_s[head, 0:tokens] = pad_lanes(head_cols(proj, flat, head))
        v_t[head, :, 0:tokens] = jnp.transpose(pad_lanes(head_cols(proj, 2 * flat, head)))
        for index, ref in enumerate(extra):
            rows = slice((index + 1) * tokens, (index + 2) * tokens)
            k_s[head, rows] = pad_lanes(head_cols(ref, 0, head))
            v_t[head, :, rows] = jnp.transpose(pad_lanes(head_cols(ref, flat, head)))

    def one_head(head, carry):
        scores = nn(k_s[head], q_t[head])
        top = jnp.max(scores, axis=0, keepdims=True)
        weights = jnp.exp2((scores - top) * scale2)
        total = jnp.sum(weights, axis=0, keepdims=True)
        weights_b = (weights * (1.0 / total)).astype(BF16)
        o_t[head] = nn(v_t[head], weights_b).astype(BF16)
        lse[head] = top * scale2 + jnp.log2(total)
        return carry

    lax.fori_loop(0, heads, one_head, 0)
    for head in range(heads):
        out[:, head * HEAD : (head + 1) * HEAD] = jnp.transpose(o_t[head])[:, :HEAD]


def attend(projected, extra, heads, scaling):
    tokens = projected.shape[0]
    keys = tokens * (1 + len(extra))
    flat = heads * HEAD
    return pl.pallas_call(
        functools.partial(attend_kernel, heads, len(extra), scaling),
        out_shape=(
            jax.ShapeDtypeStruct((tokens, flat), BF16),
            jax.ShapeDtypeStruct((heads, 1, tokens), F32),
        ),
        in_specs=[pl.BlockSpec(memory_space=pltpu.VMEM)] * (1 + len(extra)),
        out_specs=(pl.BlockSpec(memory_space=pltpu.VMEM), pl.BlockSpec(memory_space=pltpu.VMEM)),
        scratch_shapes=[
            pltpu.VMEM((heads, LANES, tokens), BF16),
            pltpu.VMEM((heads, keys, LANES), BF16),
            pltpu.VMEM((heads, LANES, keys), BF16),
            pltpu.VMEM((heads, LANES, tokens), BF16),
        ],
        cost_estimate=pl.CostEstimate(
            flops=heads * 4 * tokens * keys * LANES,
            bytes_accessed=2 * (projected.size + tokens * flat),
            transcendentals=heads * tokens * keys,
        ),
        name="attend",
    )(projected, *extra)


def attend_back_kernel(heads, spans, scaling, *refs):
    proj = refs[0]
    extra = refs[1 : 1 + spans]
    grad, attended, lse = refs[1 + spans : 4 + spans]
    count = 2 if spans else 1
    outs = refs[4 + spans : 4 + spans + count]
    q_t, q_s, k_s, k_t, v_s, d_s, d_t, delta, dq_t, dk_s, dv_s = refs[4 + spans + count :]
    tokens = proj.shape[0]
    flat = heads * HEAD
    scale2 = scaling * math.log2(math.e)
    for head in range(heads):
        q_head = pad_lanes(head_cols(proj, 0, head))
        q_s[head] = q_head
        q_t[head] = jnp.transpose(q_head)
        for index in range(1 + spans):
            rows = slice(index * tokens, (index + 1) * tokens)
            ref, base = (extra[index - 1], 0) if index else (proj, flat)
            k_head = pad_lanes(head_cols(ref, base, head))
            k_s[head, rows] = k_head
            k_t[head, :, rows] = jnp.transpose(k_head)
            v_s[head, rows] = pad_lanes(head_cols(ref, base + flat, head))
        d_head = pad_lanes(head_cols(grad, 0, head))
        d_s[head] = d_head
        d_head_t = jnp.transpose(d_head)
        d_t[head] = d_head_t
        a_head_t = jnp.transpose(pad_lanes(head_cols(attended, 0, head)))
        delta[head] = jnp.sum(
            d_head_t.astype(F32) * a_head_t.astype(F32), axis=0, keepdims=True
        )

    def one_head(head, carry):
        probs = jnp.exp2(nn(k_s[head], q_t[head]) * scale2 - lse[head])
        dv_s[head] = nn(probs.astype(BF16), d_s[head]).astype(dv_s.dtype)
        prob_grad = nn(v_s[head], d_t[head])
        score_grad = (probs * (prob_grad - delta[head]) * scaling).astype(BF16)
        dk_s[head] = nn(score_grad, q_s[head]).astype(dk_s.dtype)
        dq_t[head] = nn(k_t[head], score_grad).astype(BF16)
        return carry

    lax.fori_loop(0, heads, one_head, 0)
    for head in range(heads):
        cols = slice(head * HEAD, (head + 1) * HEAD)
        outs[0][:, cols] = jnp.transpose(dq_t[head])[:, :HEAD]
        if spans:
            outs[1][:, cols] = dk_s[head][:, :HEAD]
            outs[1][:, flat + head * HEAD : flat + (head + 1) * HEAD] = dv_s[head][:, :HEAD]
        else:
            outs[0][:, flat + head * HEAD : flat + (head + 1) * HEAD] = dk_s[head][:, :HEAD]
            outs[0][:, 2 * flat + head * HEAD : 2 * flat + (head + 1) * HEAD] = dv_s[head][:, :HEAD]


def attend_back(projected, extra, grad, attended, lse, heads, scaling):
    tokens = projected.shape[0]
    spans = len(extra)
    keys = tokens * (1 + spans)
    flat = heads * HEAD
    part = BF16 if spans == 0 else F32
    vmem = pl.BlockSpec(memory_space=pltpu.VMEM)
    if spans == 0:
        out_shape = (jax.ShapeDtypeStruct((tokens, 3 * flat), BF16),)
    else:
        out_shape = (
            jax.ShapeDtypeStruct((tokens, flat), BF16),
            jax.ShapeDtypeStruct((keys, 2 * flat), F32),
        )
    return pl.pallas_call(
        functools.partial(attend_back_kernel, heads, spans, scaling),
        out_shape=out_shape,
        in_specs=[vmem] * (4 + spans),
        out_specs=(vmem,) * len(out_shape),
        scratch_shapes=[
            pltpu.VMEM((heads, LANES, tokens), BF16),
            pltpu.VMEM((heads, tokens, LANES), BF16),
            pltpu.VMEM((heads, keys, LANES), BF16),
            pltpu.VMEM((heads, LANES, keys), BF16),
            pltpu.VMEM((heads, keys, LANES), BF16),
            pltpu.VMEM((heads, tokens, LANES), BF16),
            pltpu.VMEM((heads, LANES, tokens), BF16),
            pltpu.VMEM((heads, 1, tokens), F32),
            pltpu.VMEM((heads, LANES, tokens), BF16),
            pltpu.VMEM((heads, keys, LANES), part),
            pltpu.VMEM((heads, keys, LANES), part),
        ],
        cost_estimate=pl.CostEstimate(
            flops=heads * 10 * tokens * keys * LANES,
            bytes_accessed=2 * (2 * projected.size + 2 * tokens * flat),
            transcendentals=heads * tokens * keys,
        ),
        name="attend_back",
    )(projected, *extra, grad, attended, lse)


def around(seq, span, turn):
    base = (seq // span) * span
    return base + (seq - base + turn) % span


def halves_to_cores(grid, shard):
    mine = lax.dynamic_index_in_dim(shard, grid.core, 1, keepdims=False)
    other = lax.dynamic_index_in_dim(shard, 1 - grid.core, 1, keepdims=False)
    arrived = grid.swap_core(other)
    first = grid.core == 0
    return jnp.stack([jnp.where(first, mine, arrived), jnp.where(first, arrived, mine)])


def gather_rows(grid, stacked):
    full = lax.all_gather(stacked, ("chip", "seq"), axis=0, tiled=False)
    rows, width = stacked.shape[1:]
    full = full.reshape(grid.chips, grid.seqs, 2, rows, width)
    return full.transpose(0, 2, 1, 3, 4).reshape(grid.chips * grid.seqs * 2 * rows, width)


def local(
    inputs,
    cotangent,
    ln1_gain,
    ln1_bias,
    qkv_weight,
    qv_bias,
    out_weight,
    out_bias,
    ln2_gain,
    ln2_bias,
    up_weight,
    up_bias,
    down_weight,
    down_bias,
):
    images, _, model = inputs.shape
    grid = Grid(2 * lax.axis_size("chip"), lax.axis_size("seq"))
    span = grid.seqs // (2 * images)
    rows = qkv_weight.shape[0]
    heads = HEADS // 2
    half = model // 2
    hidden_units = up_weight.shape[1]
    ff = -(-hidden_units // (2 * LANES)) * LANES
    ff_pad = 2 * ff - hidden_units
    scaling = HEAD ** (-0.5)
    first = grid.core == 0

    x_own = to_home(grid, inputs)
    vectors = jnp.stack(
        [ln1_gain, ln1_bias, out_bias, ln2_gain, ln2_bias, down_bias, qv_bias[0], qv_bias[1]], axis=1
    )
    attn_shard = jnp.concatenate(
        [
            qkv_weight.reshape(rows, 3, 2, half).transpose(0, 2, 1, 3).reshape(rows, 2, 3 * half),
            out_weight.reshape(rows, 2, half),
            jnp.stack([vectors, vectors], axis=1),
        ],
        axis=2,
    )
    attn_set = gather_rows(grid, halves_to_cores(grid, attn_shard))
    up_shard = jnp.pad(up_weight, ((0, 0), (0, ff_pad))).reshape(rows, 2, ff)
    up_half = gather_rows(grid, halves_to_cores(grid, up_shard))
    down_shard = jnp.pad(down_weight.T, ((0, 0), (0, ff_pad))).reshape(rows, 2, ff)
    down_half = gather_rows(grid, halves_to_cores(grid, down_shard))
    cot_own = to_home(grid, cotangent)
    cot_full = grid.join(cot_own, 0)

    qkv_half = attn_set[:, : 3 * half]
    out_half = attn_set[:, 3 * half : 4 * half]
    table = jnp.transpose(attn_set[:, 4 * half :]).astype(F32)
    gain_one, shift_one, out_bias_row, gain_two, shift_two, down_bias_row = (
        table[i][None] for i in range(6)
    )
    out_full = grid.join(out_half, 1)
    qv = lax.dynamic_slice_in_dim(table[6:8], grid.core * half, half, 1)
    bias_half = jnp.concatenate([qv[0], jnp.zeros((half,), F32), qv[1]])[None]
    up_bias_half = lax.dynamic_index_in_dim(
        jnp.pad(up_bias, (0, ff_pad)).reshape(2, ff), grid.core, 0
    ).astype(F32)

    x_f = x_own.astype(F32)
    normed1, inverse1 = norm_stats(x_f)
    attn_in = grid.join((normed1 * gain_one + shift_one).astype(BF16), 0)
    projected = (nn(attn_in, qkv_half) + bias_half).astype(BF16)
    extra = tuple(
        grid.send(projected[:, half:], lambda p, c, s, r=r: (p, c, around(s, span, r)))
        for r in range(1, span)
    )
    attended_own, lse = attend(projected, extra, heads, scaling)
    attended = grid.join(attended_own, 1)
    tokens = attended.shape[0]
    own_tokens = tokens // 2
    start = grid.core * own_tokens
    attended_rows = lax.dynamic_slice_in_dim(attended, start, own_tokens, 0)
    hidden = x_f + nn(attended_rows, out_full) + out_bias_row
    normed2, inverse2 = norm_stats(hidden)
    mlp_in = grid.join((normed2 * gain_two + shift_two).astype(BF16), 0)
    pre_act = nn(mlp_in, up_half) + up_bias_half
    gelu_value, slopes = gelu_parts(pre_act)
    gelu_out = gelu_value.astype(BF16)
    down_grad = tn(cot_full, gelu_out).astype(BF16)
    gelu_grad = nn(cot_full, down_half)
    pre_grad = (gelu_grad * slopes).astype(BF16)
    up_grad = tn(mlp_in, pre_grad).astype(BF16)
    up_bias_part = jnp.sum(pre_grad.astype(F32), axis=0)

    def share(partial):
        mine = lax.dynamic_slice_in_dim(partial, start, own_tokens, 0)
        other = lax.dynamic_slice_in_dim(partial, own_tokens - start, own_tokens, 0)
        return mine + grid.swap_core(other)

    mlp_in_grad = share(nt(pre_grad, up_half))
    cot_f = cot_own.astype(F32)
    hidden_grad = cot_f + norm_back(mlp_in_grad * gain_two, normed2, inverse2)
    hidden_grad_b = grid.join(hidden_grad.astype(BF16), 0)
    out_rows = lax.dynamic_slice_in_dim(out_full, grid.core * half, half, 0)
    attended_grad = nt(hidden_grad_b, out_rows).astype(BF16)
    backward = attend_back(projected, extra, attended_grad, attended_own, lse, heads, scaling)
    if span > 1:
        q_grad, kv_parts = backward
        kv_grad = kv_parts[:tokens]
        for r in range(1, span):
            kv_grad = kv_grad + grid.send(
                kv_parts[r * tokens : (r + 1) * tokens],
                lambda p, c, s, r=r: (p, c, around(s, span, -r)),
            )
        projected_grad = jnp.concatenate([q_grad, kv_grad.astype(BF16)], axis=1)
    else:
        projected_grad = backward[0]
    result = share(nt(gelu_out, down_half)) + hidden + down_bias_row
    output = from_home(grid, result.astype(BF16), images)

    hidden_half = lax.dynamic_slice_in_dim(hidden_grad_b, grid.core * half, half, 1)
    out_grad = tn(attended, hidden_half).astype(BF16)
    qkv_grad = tn(attn_in, projected_grad).astype(BF16)
    projected_f = projected_grad.astype(F32)
    q_bias_part = jnp.sum(projected_f[:, :half], axis=0)
    v_bias_part = jnp.sum(projected_f[:, 2 * half :], axis=0)
    attn_in_grad = share(nt(projected_grad, qkv_half))
    input_grad = hidden_grad + norm_back(attn_in_grad * gain_one, normed1, inverse1)
    input_grad = from_home(grid, input_grad.astype(BF16), images)

    def placed(part):
        zero = jnp.zeros_like(part)
        return [jnp.where(first, part, zero), jnp.where(first, zero, part)]

    late = all_sum(
        grid,
        jnp.concatenate(
            [jnp.sum(cot_f, axis=0), jnp.sum(mlp_in_grad * normed2, axis=0), jnp.sum(mlp_in_grad, axis=0)]
            + [jnp.sum(hidden_grad, axis=0)]
            + placed(up_bias_part)
            + [jnp.sum(attn_in_grad * normed1, axis=0), jnp.sum(attn_in_grad, axis=0)]
            + placed(q_bias_part)
            + placed(v_bias_part)
        ),
    )
    shard = grid.flat(grid.chip, grid.core, grid.seq)

    def mine(index, base=0):
        return lax.dynamic_slice_in_dim(late, base + index * model + shard * rows, rows, 0)

    base = 4 * model + 2 * ff
    up_bias_grad = late[4 * model : 4 * model + hidden_units]

    down_pair = own_rows(grid, scatter_sum(grid, down_grad, rows))
    down_weight_grad = jnp.concatenate(down_pair, axis=1)[:, :hidden_units].T
    up_pair = own_rows(grid, scatter_sum(grid, up_grad, rows))
    up_weight_grad = jnp.concatenate(up_pair, axis=1)[:, :hidden_units]
    out_pair = own_rows(grid, scatter_sum(grid, out_grad, rows))
    out_weight_grad = jnp.concatenate(out_pair, axis=1)
    qkv_pair = own_rows(grid, scatter_sum(grid, qkv_grad, rows))
    qkv_weight_grad = (
        jnp.stack([part.reshape(rows, 3, half) for part in qkv_pair], axis=2).reshape(rows, 3 * model)
    )
    return (
        output,
        input_grad,
        mine(0, base),
        mine(1, base),
        qkv_weight_grad,
        jnp.stack([mine(2, base), mine(3, base)]),
        out_weight_grad,
        mine(3),
        mine(1),
        mine(2),
        up_weight_grad,
        up_bias_grad,
        down_weight_grad,
        mine(0),
    )


def solution(mesh):
    dps, seqs = mesh.shape["dp"], mesh.shape["seq"]
    split = jax.sharding.Mesh(mesh.devices.reshape(dps // 2, 2, seqs), AXES)
    tokens = P(("chip", "core"), "seq", None)
    vector, first_dim, last_dim = P(AXES), P(AXES, None), P(None, AXES)
    in_specs = (
        tokens,
        tokens,
        vector,
        vector,
        first_dim,
        last_dim,
        first_dim,
        vector,
        vector,
        vector,
        first_dim,
        P(),
        last_dim,
        vector,
    )
    return jax.shard_map(local, mesh=split, in_specs=in_specs, out_specs=in_specs, check_vma=False)
```
